512 devices in a mesh: member: 16 (over z), band: 32 (over y, x, core).
Axes of the slice: x: 4, y: 4, z: 16, core: 2. Of those that a mesh axis runs over, the one named last changes fastest.
Arguments:
- codes: int32 [64, 384, 6, 1408], P('member', 'band'), may hold values from -127 to 127
- exponents: int32 [64, 384, 6], P('member', 'band'), may hold values from -8 to -4
- centers: float32 [6, 256], replicated, may hold values from -3 to 3
- widths: float32 [6], replicated, may hold values from 0.01 to 0.03
Outputs:
- smoothed: bfloat16 [384, 6, 1408, 256], P('band', None, 'member')
The draws below stay inside these ranges and needn't reach their ends.
All inputs are finite; a program needn't handle non-finite values.
Results may differ from the reference program's by a relative error of at most 0.0034.
Values may be sent and summed in bfloat16 or wider, within the bound.
No kernel may reach another device: no remote copies, remote signals or barrier semaphores. Data moves between devices by JAX's collectives and lax.ppermute only.
A program may use at most 64 MiB of HBM per device.

```python
import math
import jax
import jax.numpy as jnp
from jax import lax

MEMBERS = 64
VARS = 6
BINS = 256
NLAT = 384
LON = 1408


def plant(result, rng, low, largest):
    place = [jax.random.randint(jax.random.fold_in(rng, axis), (), 0, length) for axis, length in enumerate(result.shape)]
    widest = result.shape.index(max(result.shape))
    beside = place[:widest] + [(place[widest] + 1) % result.shape[widest]] + place[widest + 1:]
    return result.at[tuple(place)].set(low).at[tuple(beside)].set(largest)


def setup_inputs(seed: int = 0) -> dict:
    streams_of = jax.random.split(jax.random.key(seed), 5)
    codes = plant(jax.random.randint(streams_of[0], (MEMBERS, NLAT, VARS, LON), -127, 128), jax.random.fold_in(streams_of[0], 1), -127, 127).astype(jnp.int32)
    exponents = plant(jax.random.randint(streams_of[1], (MEMBERS, NLAT, VARS), -8, -3), jax.random.fold_in(streams_of[1], 1), -8, (-3) - 1).astype(jnp.int32)
    centers = jnp.clip(jax.random.uniform(streams_of[2], (VARS, BINS), jnp.float32, -3.0, 3.0), -3.0, 3.0)
    widths = jnp.clip(jnp.exp(jax.random.uniform(streams_of[3], (VARS,), jnp.float32, math.log(0.01), math.log(0.03))), 0.01, 0.03)
    return dict(codes=codes, exponents=exponents, centers=centers, widths=widths)


def var_density(item, center, width):
    field = item.astype(jnp.float32)
    scaled = (center[None, None, None, :] - field[:, :, :, None]) / width
    total = lax.optimization_barrier(jnp.sum(jnp.exp(-0.5 * scaled * scaled), axis=0))
    return total / (field.shape[0] * width * math.sqrt(2.0 * math.pi))

def block_density(values, centers, widths):
    items = jnp.transpose(values, (2, 0, 1, 3))
    dens = lax.map(lambda t: var_density(t[0], t[1], t[2]), (items, centers, widths))
    return jnp.transpose(dens, (1, 0, 2, 3)).astype(jnp.bfloat16)

def reference(codes, exponents, centers, widths):
    scale = jnp.exp2(exponents.astype(jnp.float32))
    values = (codes.astype(jnp.float32) * scale[..., None]).astype(jnp.bfloat16)
    dens = block_density(values, centers, widths).astype(jnp.float32)
    padded = jnp.pad(dens, ((2, 2), (0, 0), (2, 2), (0, 0)))
    lat_sum = padded[0:NLAT] + padded[1:NLAT + 1] + padded[2:NLAT + 2] + padded[3:NLAT + 3] + padded[4:NLAT + 4]
    total = lat_sum[:, :, 0:LON] + lat_sum[:, :, 1:LON + 1] + lat_sum[:, :, 2:LON + 2] + lat_sum[:, :, 3:LON + 3] + lat_sum[:, :, 4:LON + 4]
    return (total / 25.0).astype(jnp.bfloat16)
```

```python
import math

import jax
import jax.numpy as jnp
from jax import lax
from jax.experimental import pallas as pl
from jax.experimental.pallas import tpu as pltpu
from jax.sharding import PartitionSpec as P

F32, BF16, I32 = jnp.float32, jnp.bfloat16, jnp.int32
SECTORS, ROWS, VARS, CELLS, BINS = 16, 12, 6, 88, 256
WIDE = 96
LEVELS = 5
FEATURES = LEVELS * 256


def packed_codes(codes, exponents):
    c = codes.astype(BF16)
    c = jnp.pad(c, ((0, 0), (0, 0), (0, 0), (2, WIDE - CELLS - 2)))
    s = jnp.stack([c[..., CELLS * j : CELLS * j + WIDE] for j in range(SECTORS)])
    s = s.reshape(SECTORS, 4, 3, 4, VARS, WIDE)
    s = jnp.transpose(s, (0, 2, 4, 1, 3, 5)).reshape(SECTORS, 3, VARS, 4, 3, 128)
    s = jnp.transpose(s, (0, 1, 4, 2, 3, 5)).reshape(SECTORS, 216, 128)
    e = jnp.pad((exponents + 8).astype(BF16).reshape(-1), (0, 8 * 128 - 288))
    e = jnp.broadcast_to(e.reshape(1, 8, 128), (SECTORS, 8, 128))
    return jnp.concatenate([s, e], axis=1)


def levels_of(rows):
    n = rows.shape[0]
    return rows.reshape(n, 8 * 128)[:, :288].astype(I32).reshape(n * 4, ROWS, VARS)


def kernel_table(centers, widths):
    f = jnp.arange(FEATURES)
    level, byte, word = f // 256, (f // 64) % 4, f % 64
    x = (4 * word + byte - 128).astype(F32) * jnp.exp2((level - 8).astype(F32))
    d = (centers[:, :, None] - x[None, None, :]) / widths[:, None, None]
    return jnp.exp(-0.5 * d * d).astype(BF16)


def density_kernel(lev, scale, flag, r_ref, fr_ref, fl_ref, t_ref, s_ref, o_ref, hi, val, acc0, acc1, a_ref, p_ref):
    step = pl.program_id(0)
    lane = lax.broadcasted_iota(I32, (SECTORS, 8, 128), 2)

    def tile(ref, k):
        start = pl.multiple_of(k * 24 + step * 8, 8)
        return ref[:, pl.ds(start, 8), :].astype(F32)

    def put(rr, x):
        c = x.astype(I32) + 128
        hi[rr] = lax.shift_right_logical(c, 2)
        val[rr] = lax.shift_left(jnp.ones_like(c), (c & 3) * 8)

    for g in range(4):
        if g < 3:
            t0, t1, t2 = (tile(r_ref, g * 3 + k) for k in range(3))
        else:
            t0, t2 = tile(fr_ref, 0), tile(fl_ref, 1)
            t1 = jnp.where(lane < 64, tile(fr_ref, 1), tile(fl_ref, 0))
        put(4 * g, t0)
        put(4 * g + 1, jnp.where(lane < 32, pltpu.roll(t0, 32, 2), pltpu.roll(t1, 32, 2)))
        put(4 * g + 2, jnp.where(lane < 64, pltpu.roll(t1, 64, 2), pltpu.roll(t2, 64, 2)))
        put(4 * g + 3, pltpu.roll(t2, 96, 2))

    words = lax.broadcasted_iota(I32, (64, 128), 0)

    @pl.loop(0, 16)
    def _(job):
        vv = job // 8
        pair = (job % 8) * 2
        accs = (acc0, acc1)
        for acc in accs:
            acc[...] = jnp.zeros_like(acc)

        @pl.loop(0, SECTORS)
        def _(src):
            for mm in range(4):
                for q in range(2):
                    e = lev[(step * 2 + vv) * 16 + pair + q, src * 4 + mm]
                    row = pl.ds(vv * 4 + mm, 1)
                    h = jnp.broadcast_to(hi[pair + q, src, row], (64, 128))
                    v = jnp.broadcast_to(val[pair + q, src, row], (64, 128))
                    pltpu.store(accs[q].at[e], accs[q][e] + v, mask=h == words)

        for q in range(2):
            for e in range(LEVELS):
                a = accs[q][e]
                for j in range(4):
                    n = lax.shift_right_logical(a, 8 * j) & 255
                    a_ref[e * 256 + j * 64 : e * 256 + j * 64 + 64, q * 128 : q * 128 + 128] = n.astype(F32).astype(BF16)
        d = jnp.dot(t_ref[vv], a_ref[...], preferred_element_type=F32).astype(BF16)
        for q in range(2):
            rr = pair + q
            p = lax.dot_general(s_ref[...], d[:, q * 128 : q * 128 + 128], (((1,), (1,)), ((), ())), preferred_element_type=F32)
            p_ref[vv, lax.rem(rr + 2, 16)] = p * flag[rr]

    for vv in range(2):

        @pl.loop(0, ROWS)
        def _(r):
            total = p_ref[vv, r]
            for k in range(1, 5):
                total = total + p_ref[vv, r + k]
            o_ref[r, vv] = (total[:CELLS] * scale[step * 2 + vv]).astype(BF16)


def densities(lev, scale, flag, owned, right, left, table, window):
    smem = pl.BlockSpec(memory_space=pltpu.SMEM)
    vmem = pl.BlockSpec(memory_space=pltpu.VMEM)
    return pl.pallas_call(
        density_kernel,
        out_shape=jax.ShapeDtypeStruct((ROWS, VARS, CELLS, BINS), BF16),
        grid=(3,),
        in_specs=[smem, smem, smem, vmem, vmem, vmem, pl.BlockSpec((2, BINS, FEATURES), lambda i: (i, 0, 0)), vmem],
        out_specs=pl.BlockSpec((ROWS, 2, CELLS, BINS), lambda i: (0, i, 0, 0)),
        scratch_shapes=[
            pltpu.VMEM((16, SECTORS, 8, 128), I32),
            pltpu.VMEM((16, SECTORS, 8, 128), I32),
            pltpu.VMEM((LEVELS, 64, 128), I32),
            pltpu.VMEM((LEVELS, 64, 128), I32),
            pltpu.VMEM((FEATURES, 256), BF16),
            pltpu.VMEM((2, 16, WIDE, BINS), F32),
        ],
        compiler_params=pltpu.CompilerParams(vmem_limit_bytes=56 << 20),
        cost_estimate=pl.CostEstimate(flops=10**10, bytes_accessed=10**7, transcendentals=0),
    )(lev, scale, flag, owned, right, left, table, window)


def shards(codes, exponents, centers, widths):
    sector, band = lax.axis_index("member"), lax.axis_index("band")
    bands = lax.axis_size("band")
    owned = lax.all_to_all(packed_codes(codes, exponents), "member", split_axis=0, concat_axis=0, tiled=True)
    table = kernel_table(centers, widths)
    head = jnp.concatenate([owned[:, 0:48], owned[:, 216:224]], axis=1)
    right = lax.ppermute(head, "band", [(i + 1, i) for i in range(bands - 1)])
    left = lax.ppermute(owned[:, 168:224], "band", [(i, i + 1) for i in range(bands - 1)])
    lev = jnp.concatenate(
        [levels_of(owned[:, 216:224]), levels_of(right[:, 48:56])[:, :2], levels_of(left[:, 48:56])[:, 10:]], axis=1
    )
    lev = jnp.transpose(lev, (2, 1, 0)).reshape(VARS * 16, 64)
    scale = 1.0 / (25.0 * 64.0 * math.sqrt(2.0 * math.pi) * widths)
    rr = jnp.arange(16)
    flag = jnp.where(rr < 12, True, jnp.where(rr < 14, band < bands - 1, band > 0)).astype(F32)
    out_l, lane = jnp.arange(WIDE)[:, None], jnp.arange(128)[None, :]
    cell = sector * CELLS + lane - 2
    inside = (lane >= out_l) & (lane <= out_l + 4) & (cell >= 0) & (cell < SECTORS * CELLS) & (out_l < CELLS)
    return densities(lev, scale, flag, owned, right, left, table, inside.astype(BF16))


def solution(mesh):
    return jax.shard_map(
        shards,
        mesh=mesh,
        in_specs=(P("member", "band", None, None), P("member", "band", None), P(), P()),
        out_specs=P("band", None, "member", None),
        check_vma=False,
    )
```

```python
import math

import jax
import jax.numpy as jnp
from jax import lax
from jax.experimental import pallas as pl
from jax.experimental.pallas import tpu as pltpu
from jax.sharding import PartitionSpec as P

F32, BF16, I32 = jnp.float32, jnp.bfloat16, jnp.int32
SECTORS, ROWS, VARS, CELLS, BINS = 16, 12, 6, 88, 256
WIDE = 96
LEVELS = 5
FEATURES = LEVELS * 256
QUAD = 4
SMEM = pl.BlockSpec(memory_space=pltpu.SMEM)
VMEM = pl.BlockSpec(memory_space=pltpu.VMEM)


def packed_codes(codes):
    groups = codes.shape[1] // 4
    c = jnp.pad(codes.astype(BF16), ((0, 0), (0, 0), (0, 0), (2, WIDE - CELLS - 2)))
    s = jnp.stack([c[..., CELLS * j : CELLS * j + WIDE] for j in range(SECTORS)])
    s = s.reshape(SECTORS, 4, groups, 4, VARS, WIDE)
    s = jnp.transpose(s, (0, 2, 4, 1, 3, 5)).reshape(SECTORS, groups, VARS, 4, 3, 128)
    return jnp.transpose(s, (0, 1, 4, 2, 3, 5)).reshape(SECTORS, groups * 72, 128)


def packed_levels(exponents):
    e = jnp.pad((exponents + 8).astype(BF16).reshape(4, ROWS * VARS), ((0, 4), (0, 128 - ROWS * VARS)))
    return jnp.broadcast_to(e[None], (SECTORS, 8, 128))


def levels_of(rows):
    return rows[:, :4, : ROWS * VARS].astype(I32).reshape(4 * SECTORS, ROWS * VARS)


def kernel_table(centers, widths):
    f = jnp.arange(FEATURES)
    level, byte, word = f // 256, (f // 64) % 4, f % 64
    x = (4 * word + byte - 128).astype(F32) * jnp.exp2((level - 8).astype(F32))
    d = (centers[:, :, None] - x[None, None, :]) / widths[:, None, None]
    return jnp.exp(-0.5 * d * d).astype(BF16)


def unpack(quad, t0, t1, t2, word, bit):
    lane = lax.broadcasted_iota(I32, (SECTORS, 8, 128), 2)

    def put(k, x):
        c = x.astype(I32) + 128
        word[quad * 4 + k] = lax.shift_right_logical(c, 2)
        bit[quad * 4 + k] = lax.shift_left(jnp.ones_like(c), (c & 3) * 8)

    put(0, t0)
    put(1, jnp.where(lane < 32, pltpu.roll(t0, 32, 2), pltpu.roll(t1, 32, 2)))
    put(2, jnp.where(lane < 64, pltpu.roll(t1, 64, 2), pltpu.roll(t2, 64, 2)))
    put(3, pltpu.roll(t2, 96, 2))


def tile_of(ref, k):
    start = pl.multiple_of(k * 24 + pl.program_id(0) * 8, 8)
    return ref[:, pl.ds(start, 8), :].astype(F32)


def row_sums(lev, t_ref, s_ref, word, bit, a_ref, accs, put):
    step = pl.program_id(0)
    words = lax.broadcasted_iota(I32, (64, 128), 0)
    for acc in accs:
        acc[...] = jnp.zeros_like(acc)

    @pl.loop(0, 4)
    def _(job):
        vv = job // 2
        first = (job % 2) * QUAD

        @pl.loop(0, SECTORS // 4)
        def _(block):
            for k in range(16):
                src, mm = block * 4 + k // 4, k % 4
                for q in range(QUAD):
                    e = lev[src * 4 + mm, (first + q) * VARS + step * 2 + vv]
                    at = pl.ds(vv * 4 + mm, 1)
                    h = jnp.broadcast_to(word[first + q, src, at], (64, 128))
                    v = jnp.broadcast_to(bit[first + q, src, at], (64, 128))
                    accs[q][e] = accs[q][e] + jnp.where(h == words, v, 0)

        for q in range(QUAD):
            for e in range(LEVELS):
                a = accs[q][e]
                accs[q][e] = jnp.zeros_like(a)
                for j in range(4):
                    n = lax.shift_right_logical(a, 8 * j) & 255
                    a_ref[e * 256 + j * 64 : e * 256 + j * 64 + 64, q * 128 : q * 128 + 128] = n.astype(F32).astype(BF16)

        d = jnp.dot(t_ref[vv], a_ref[...], preferred_element_type=F32).astype(BF16)
        for q in range(QUAD):
            p = lax.dot_general(s_ref[...], d[:, q * 128 : q * 128 + 128], (((1,), (1,)), ((), ())), preferred_element_type=F32)
            put(first + q, vv, p)


def outer_kernel(lev, r_ref, t_ref, s_ref, p_ref, word, bit, a_ref, *accs):
    for quad in range(2):
        unpack(quad, *(tile_of(r_ref, quad * 3 + k) for k in range(3)), word, bit)

    def put(k, vv, p):
        p_ref[k, vv] = p

    row_sums(lev, t_ref, s_ref, word, bit, a_ref, accs, put)


def inner_kernel(lev, scale, flag, r_ref, fr_ref, fl_ref, p_ref, t_ref, s_ref, o_ref, own, word, bit, a_ref, *accs):
    lane = lax.broadcasted_iota(I32, (SECTORS, 8, 128), 2)
    unpack(0, tile_of(fr_ref, 0), jnp.where(lane < 64, tile_of(fr_ref, 1), tile_of(fl_ref, 0)), tile_of(fl_ref, 1), word, bit)
    unpack(1, *(tile_of(r_ref, k) for k in range(3)), word, bit)

    def put(k, vv, p):
        own[k, vv] = p * flag[k]

    row_sums(lev, t_ref, s_ref, word, bit, a_ref, accs, put)
    rows = [(own, 2), (own, 3)] + [(p_ref, k) for k in range(4)] + [(own, k) for k in range(4, 8)]
    rows += [(p_ref, k) for k in range(4, 8)] + [(own, 0), (own, 1)]

    @pl.loop(0, 2)
    def _(vv):
        factor = scale[pl.program_id(0) * 2 + vv]
        for r in range(ROWS):
            ref, k = rows[r]
            total = ref[k, vv]
            for ref, k in rows[r + 1 : r + 5]:
                total = total + ref[k, vv]
            o_ref[r, vv] = (total[:CELLS] * factor).astype(BF16)


SCRATCH = [
    pltpu.VMEM((8, SECTORS, 8, 128), I32),
    pltpu.VMEM((8, SECTORS, 8, 128), I32),
    pltpu.VMEM((FEATURES, QUAD * 128), BF16),
] + [pltpu.VMEM((LEVELS, 64, 128), I32)] * QUAD
PARAMS = dict(
    compiler_params=pltpu.CompilerParams(vmem_limit_bytes=48 << 20),
    cost_estimate=pl.CostEstimate(flops=10**10, bytes_accessed=10**7, transcendentals=0),
)
TABLE = pl.BlockSpec((2, BINS, FEATURES), lambda i: (i, 0, 0))
SUMS = pl.BlockSpec((8, 2, WIDE, BINS), lambda i: (0, i, 0, 0))


def outer_rows(lev, owned, table, window):
    return pl.pallas_call(
        outer_kernel,
        out_shape=jax.ShapeDtypeStruct((8, VARS, WIDE, BINS), F32),
        grid=(3,),
        in_specs=[SMEM, VMEM, TABLE, VMEM],
        out_specs=SUMS,
        scratch_shapes=SCRATCH,
        **PARAMS,
    )(lev, owned, table, window)


def all_rows(lev, scale, flag, owned, right, left, outer, table, window):
    return pl.pallas_call(
        inner_kernel,
        out_shape=jax.ShapeDtypeStruct((ROWS, VARS, CELLS, BINS), BF16),
        grid=(3,),
        in_specs=[SMEM, SMEM, SMEM, VMEM, VMEM, VMEM, SUMS, TABLE, VMEM],
        out_specs=pl.BlockSpec((ROWS, 2, CELLS, BINS), lambda i: (0, i, 0, 0)),
        scratch_shapes=[pltpu.VMEM((8, 2, WIDE, BINS), F32)] + SCRATCH,
        **PARAMS,
    )(lev, scale, flag, owned, right, left, outer, table, window)


def exchanged(x):
    return lax.all_to_all(x, "member", split_axis=0, concat_axis=0, tiled=True)


def shards(codes, exponents, centers, widths):
    sector, band = lax.axis_index("member"), lax.axis_index("band")
    bands = lax.axis_size("band")
    edges = jnp.concatenate([codes[:, :4], codes[:, 8:]], axis=1)
    first = exchanged(jnp.concatenate([packed_codes(edges), packed_levels(exponents)], axis=1))
    second = exchanged(packed_codes(codes[:, 4:8]))
    table = kernel_table(centers, widths)
    head = jnp.concatenate([first[:, :48], first[:, 144:]], axis=1)
    right = lax.ppermute(head, "band", [(i + 1, i) for i in range(bands - 1)])
    left = lax.ppermute(first[:, 96:], "band", [(i, i + 1) for i in range(bands - 1)])
    lev = levels_of(first[:, 144:])
    outer_lev = jnp.concatenate([lev[:, :24], lev[:, 48:]], axis=1)
    inner_lev = jnp.concatenate([levels_of(right[:, 48:])[:, :12], levels_of(left[:, 48:])[:, 60:], lev[:, 24:48]], axis=1)
    scale = 1.0 / (25.0 * 64.0 * math.sqrt(2.0 * math.pi) * widths)
    k = jnp.arange(8)
    flag = jnp.where(k >= 4, True, jnp.where(k < 2, band < bands - 1, band > 0)).astype(F32)
    out_l, lane = jnp.arange(WIDE)[:, None], jnp.arange(128)[None, :]
    cell = sector * CELLS + lane - 2
    window = (lane >= out_l) & (lane <= out_l + 4) & (cell >= 0) & (cell < SECTORS * CELLS) & (out_l < CELLS)
    window = window.astype(BF16)
    outer = outer_rows(outer_lev, first, table, window)
    return all_rows(inner_lev, scale, flag, second, right, left, outer, table, window)


def solution(mesh):
    return jax.shard_map(
        shards,
        mesh=mesh,
        in_specs=(P("member", "band", None, None), P("member", "band", None), P(), P()),
        out_specs=P("band", None, "member", None),
        check_vma=False,
    )
```

```python
import math

import jax
import jax.numpy as jnp
from jax import lax
from jax.experimental import pallas as pl
from jax.experimental.pallas import tpu as pltpu
from jax.sharding import PartitionSpec as P

F32, BF16, I32 = jnp.float32, jnp.bfloat16, jnp.int32
SECTORS, ROWS, VARS, CELLS, BINS = 16, 12, 6, 88, 256
WIDE = 96
LEVELS = 5
FEATURES = LEVELS * 256
GROUPS = 1
SPLIT = 6
JOINED = 4
SMEM = pl.BlockSpec(memory_space=pltpu.SMEM)
VMEM = pl.BlockSpec(memory_space=pltpu.VMEM)


def packed_codes(codes):
    groups = codes.shape[1] // 4
    c = jnp.pad(codes.astype(BF16), ((0, 0), (0, 0), (0, 0), (2, WIDE - CELLS - 2)))
    s = jnp.stack([c[..., CELLS * j : CELLS * j + WIDE] for j in range(SECTORS)])
    s = s.reshape(SECTORS, 4, groups, 4, VARS, WIDE)
    s = jnp.transpose(s, (0, 2, 4, 1, 3, 5)).reshape(SECTORS, groups, VARS, 4, 3, 128)
    return jnp.transpose(s, (0, 1, 4, 2, 3, 5)).reshape(SECTORS, groups * 72, 128)


def packed_levels(exponents):
    e = jnp.pad((exponents + 8).astype(BF16).reshape(4, ROWS * VARS), ((0, 4), (0, 128 - ROWS * VARS)))
    return jnp.broadcast_to(e[None], (SECTORS, 8, 128))


def levels_of(rows):
    return rows[:, :4, : ROWS * VARS].astype(I32).reshape(4 * SECTORS, ROWS * VARS)


def kernel_table(centers, widths):
    f = jnp.arange(FEATURES)
    level, byte, word = f // 256, (f // 64) % 4, f % 64
    x = (4 * word + byte - 128).astype(F32) * jnp.exp2((level - 8).astype(F32))
    d = (centers[:, :, None] - x[None, None, :]) / widths[:, None, None]
    return jnp.exp(-0.5 * d * d).astype(BF16)


def unpack(quad, t0, t1, t2, word, bit):
    lane = lax.broadcasted_iota(I32, (SECTORS, 8, 128), 2)

    def put(k, x):
        c = x.astype(I32) + 128
        word[quad * 4 + k] = lax.shift_right_logical(c, 2)
        bit[quad * 4 + k, 0] = lax.shift_left(jnp.ones_like(c), (c & 3) * 8)

    put(0, t0)
    put(1, jnp.where(lane < 32, pltpu.roll(t0, 32, 2), pltpu.roll(t1, 32, 2)))
    put(2, jnp.where(lane < 64, pltpu.roll(t1, 64, 2), pltpu.roll(t2, 64, 2)))
    put(3, pltpu.roll(t2, 96, 2))


def tile_of(ref, k):
    start = pl.multiple_of(k * 24 + pl.program_id(0) * 8, 8)
    return ref[:, pl.ds(start, 8), :].astype(F32)


def row_sums(chains, lev, t_ref, s_ref, word, bit, a_ref, accs, put):
    step = pl.program_id(0)
    part = 64 // GROUPS
    words = lax.broadcasted_iota(I32, (part, 128), 0)

    @pl.loop(0, SECTORS)
    def _(src):
        for mm in range(4):
            for acc, (slot, vv) in zip(accs, chains):
                e = lev[src * 4 + mm, slot * VARS + step * 2 + vv]
                at = pl.ds(vv * 4 + mm, 1)
                here = jnp.broadcast_to(word[slot, src, at], (part, 128)) == words
                for g in range(GROUPS):
                    v = jnp.broadcast_to(bit[slot, g, src, at], (part, 128))
                    span = pl.ds(g * part, part)
                    acc[e, span] = acc[e, span] + jnp.where(here, v, 0)

    for k in range(0, 8, JOINED):
        for c in range(k, k + JOINED):
            for e in range(LEVELS):
                a = accs[c][e]
                accs[c][e] = jnp.zeros_like(a)
                for j in range(4):
                    n = lax.shift_right_logical(a, 8 * j) & 255
                    a_ref[c, e * 256 + j * 64 : e * 256 + j * 64 + 64] = n.astype(F32).astype(BF16)
        counts = jnp.concatenate([a_ref[c] for c in range(k, k + JOINED)], axis=1)
        d = jnp.dot(t_ref[chains[k][1]], counts, preferred_element_type=F32).astype(BF16)
        for i in range(JOINED):
            p = lax.dot_general(s_ref[...], d[:, i * 128 : i * 128 + 128], (((1,), (1,)), ((), ())), preferred_element_type=F32)
            put(*chains[k + i], p)


def outer_kernel(lev, r_ref, t_ref, s_ref, p_ref, part_ref, head_ref, tail_ref, word, bit, a_ref, *accs):
    for quad in range(2):
        unpack(quad, *(tile_of(r_ref, quad * 3 + k) for k in range(3)), word, bit)
    for acc in accs:
        acc[...] = jnp.zeros_like(acc)

    def put(k, vv, p):
        p_ref[k, vv] = p

    @pl.loop(0, 2)
    def _(vv):
        row_sums([(k, vv) for k in range(8)], lev, t_ref, s_ref, word, bit, a_ref, accs, put)
        for k in range(2):
            head_ref[k, vv] = p_ref[k, vv, :CELLS].astype(BF16)
            tail_ref[k, vv] = p_ref[6 + k, vv, :CELLS].astype(BF16)
        low = p_ref[0, vv, :CELLS] + p_ref[1, vv, :CELLS] + p_ref[2, vv, :CELLS]
        part_ref[0, vv] = low
        part_ref[1, vv] = low + p_ref[3, vv, :CELLS]
        high = p_ref[5, vv, :CELLS] + p_ref[6, vv, :CELLS] + p_ref[7, vv, :CELLS]
        part_ref[2, vv] = high + p_ref[4, vv, :CELLS]
        part_ref[3, vv] = high


def inner_kernel(lev, scale, r_ref, p_ref, t_ref, s_ref, o_ref, own, word, bit, a_ref, *accs):
    unpack(0, *(tile_of(r_ref, k) for k in range(3)), word, bit)
    for acc in accs:
        acc[...] = jnp.zeros_like(acc)

    def put(k, vv, p):
        own[k, vv] = p

    row_sums([(k, vv) for vv in range(2) for k in range(4)], lev, t_ref, s_ref, word, bit, a_ref, accs, put)
    rows = [(p_ref, k) for k in range(4)] + [(own, k) for k in range(4)] + [(p_ref, k) for k in range(4, 8)]

    @pl.loop(0, 2)
    def _(vv):
        factor = scale[pl.program_id(0) * 2 + vv]
        for r in range(8):
            ref, k = rows[r]
            total = ref[k, vv]
            for ref, k in rows[r + 1 : r + 5]:
                total = total + ref[k, vv]
            o_ref[r + 2, vv] = (total[:CELLS] * factor).astype(BF16)


def edge_kernel(scale, part_ref, right_ref, left_ref, done_ref, o_ref):
    end, step = pl.program_id(1), pl.program_id(0)
    for vv in range(2):
        factor = scale[step * 2 + vv]

        @pl.when(end == 0)
        def _():
            last = left_ref[1, vv].astype(F32)
            o_ref[0, vv] = ((part_ref[0, vv] + left_ref[0, vv].astype(F32) + last) * factor).astype(BF16)
            o_ref[1, vv] = ((part_ref[1, vv] + last) * factor).astype(BF16)

        @pl.when(end == 1)
        def _():
            next_ = right_ref[0, vv].astype(F32)
            o_ref[0, vv] = ((part_ref[0, vv] + next_) * factor).astype(BF16)
            o_ref[1, vv] = ((part_ref[1, vv] + next_ + right_ref[1, vv].astype(F32)) * factor).astype(BF16)


def scratch(slots):
    return [
        pltpu.VMEM((slots, SECTORS, 8, 128), I32),
        pltpu.VMEM((slots, GROUPS, SECTORS, 8, 128), I32),
        pltpu.VMEM((8, FEATURES, 128), BF16),
    ] + [pltpu.VMEM((LEVELS, 64, 128), I32)] * 8


PARAMS = dict(compiler_params=pltpu.CompilerParams(vmem_limit_bytes=52 << 20))
COST = pl.CostEstimate(flops=10**10, bytes_accessed=10**7, transcendentals=0)
TABLE = pl.BlockSpec((2, BINS, FEATURES), lambda i: (i, 0, 0))


def blocks(rows, cells=CELLS):
    return pl.BlockSpec((rows, 2, cells, BINS), lambda i: (0, i, 0, 0))


def outer_rows(lev, owned, table, window):
    shape = lambda rows, cells, dtype: jax.ShapeDtypeStruct((rows, VARS, cells, BINS), dtype)
    return pl.pallas_call(
        outer_kernel,
        out_shape=[shape(8, WIDE, F32), shape(4, CELLS, F32), shape(2, CELLS, BF16), shape(2, CELLS, BF16)],
        grid=(3,),
        in_specs=[SMEM, VMEM, TABLE, VMEM],
        out_specs=[blocks(8, WIDE), blocks(4), blocks(2), blocks(2)],
        scratch_shapes=scratch(8),
        cost_estimate=COST,
        **PARAMS,
    )(lev, owned, table, window)


def inner_rows(lev, scale, owned, outer, table, window):
    return pl.pallas_call(
        inner_kernel,
        out_shape=jax.ShapeDtypeStruct((ROWS, VARS, CELLS, BINS), BF16),
        grid=(3,),
        in_specs=[SMEM, SMEM, VMEM, blocks(8, WIDE), TABLE, VMEM],
        out_specs=blocks(ROWS),
        scratch_shapes=[pltpu.VMEM((4, 2, WIDE, BINS), F32)] + scratch(4),
        cost_estimate=COST,
        **PARAMS,
    )(lev, scale, owned, outer, table, window)


def edge_rows(scale, part, right, left, done):
    def block(where):
        return pl.BlockSpec((2, 2, CELLS, BINS), where)

    return pl.pallas_call(
        edge_kernel,
        out_shape=jax.ShapeDtypeStruct((ROWS, VARS, CELLS, BINS), BF16),
        grid=(3, 2),
        in_specs=[
            SMEM,
            block(lambda i, end: (end, i, 0, 0)),
            block(lambda i, end: (0, i, 0, 0)),
            block(lambda i, end: (0, i, 0, 0)),
            pl.BlockSpec(memory_space=pl.ANY),
        ],
        out_specs=block(lambda i, end: (end * 5, i, 0, 0)),
        input_output_aliases={4: 0},
        cost_estimate=pl.CostEstimate(flops=10**6, bytes_accessed=10**6, transcendentals=0),
        **PARAMS,
    )(scale, part, right, left, done)


def exchanged(x):
    return lax.all_to_all(x, "member", split_axis=0, concat_axis=0, tiled=True)


def shards(codes, exponents, centers, widths):
    sector = lax.axis_index("member")
    bands = lax.axis_size("band")
    edges = jnp.concatenate([codes[:, :4], codes[:, 8:]], axis=1)
    first = exchanged(jnp.concatenate([packed_codes(edges), packed_levels(exponents)], axis=1))
    second = exchanged(packed_codes(codes[:, 4:8]))
    table = kernel_table(centers, widths)
    lev = levels_of(first[:, 144:])
    outer_lev = jnp.concatenate([lev[:, :24], lev[:, 48:]], axis=1)
    scale = 1.0 / (25.0 * 64.0 * math.sqrt(2.0 * math.pi) * widths)
    out_l, lane = jnp.arange(WIDE)[:, None], jnp.arange(128)[None, :]
    cell = sector * CELLS + lane - 2
    window = (lane >= out_l) & (lane <= out_l + 4) & (cell >= 0) & (cell < SECTORS * CELLS) & (out_l < CELLS)
    window = window.astype(BF16)
    outer, part, head, tail = outer_rows(outer_lev, first, table, window)
    right = lax.ppermute(head, "band", [(i + 1, i) for i in range(bands - 1)])
    left = lax.ppermute(tail, "band", [(i, i + 1) for i in range(bands - 1)])
    done = inner_rows(lev[:, 24:48], scale, second, outer, table, window)
    return edge_rows(scale, part, right, left, done)


def solution(mesh):
    return jax.shard_map(
        shards,
        mesh=mesh,
        in_specs=(P("member", "band", None, None), P("member", "band", None), P(), P()),
        out_specs=P("band", None, "member", None),
        check_vma=False,
    )
```

```python
import math

import jax
import jax.numpy as jnp
from jax import lax
from jax.experimental import pallas as pl
from jax.experimental.pallas import tpu as pltpu
from jax.sharding import PartitionSpec as P

F32, BF16, I32 = jnp.float32, jnp.bfloat16, jnp.int32
SECTORS, ROWS, VARS, CELLS, BINS = 16, 12, 6, 88, 256
WIDE = 96
EDGE_MIB = 32
LEVELS = 5
FEATURES = LEVELS * 256
GROUPS = 1
SPLIT = 6
SMEM = pl.BlockSpec(memory_space=pltpu.SMEM)
VMEM = pl.BlockSpec(memory_space=pltpu.VMEM)


def packed_codes(codes):
    groups = codes.shape[1] // 4
    c = jnp.pad(codes.astype(BF16), ((0, 0), (0, 0), (0, 0), (2, WIDE - CELLS - 2)))
    s = jnp.stack([c[..., CELLS * j : CELLS * j + WIDE] for j in range(SECTORS)])
    s = s.reshape(SECTORS, 4, groups, 4, VARS, WIDE)
    s = jnp.transpose(s, (0, 2, 4, 1, 3, 5)).reshape(SECTORS, groups, VARS, 4, 3, 128)
    return jnp.transpose(s, (0, 1, 4, 2, 3, 5)).reshape(SECTORS, groups * 72, 128)


def packed_levels(exponents):
    e = jnp.pad((exponents + 8).astype(BF16).reshape(4, ROWS * VARS), ((0, 4), (0, 128 - ROWS * VARS)))
    return jnp.broadcast_to(e[None], (SECTORS, 8, 128))


def levels_of(rows):
    return rows[:, :4, : ROWS * VARS].astype(I32).reshape(4 * SECTORS, ROWS * VARS)


def kernel_table(centers, widths):
    f = jnp.arange(FEATURES)
    level, byte, word = f // 256, (f // 64) % 4, f % 64
    x = (4 * word + byte - 128).astype(F32) * jnp.exp2((level - 8).astype(F32))
    d = (centers[:, :, None] - x[None, None, :]) / widths[:, None, None]
    return jnp.exp(-0.5 * d * d).astype(BF16)


def unpack(quad, t0, t1, t2, word, bit):
    lane = lax.broadcasted_iota(I32, (SECTORS, 8, 128), 2)

    def put(k, x):
        c = x.astype(I32) + 128
        word[quad * 4 + k] = lax.shift_right_logical(c, 2)
        bit[quad * 4 + k, 0] = lax.shift_left(jnp.ones_like(c), (c & 3) * 8)

    put(0, t0)
    put(1, jnp.where(lane < 32, pltpu.roll(t0, 32, 2), pltpu.roll(t1, 32, 2)))
    put(2, jnp.where(lane < 64, pltpu.roll(t1, 64, 2), pltpu.roll(t2, 64, 2)))
    put(3, pltpu.roll(t2, 96, 2))


def tile_of(ref, k):
    start = pl.multiple_of(k * 24 + pl.program_id(0) * 8, 8)
    return ref[:, pl.ds(start, 8), :].astype(F32)


def row_sums(chains, joined, lev, t_ref, s_ref, word, bit, a_ref, accs, put):
    step = pl.program_id(0)
    part = 64 // GROUPS
    words = lax.broadcasted_iota(I32, (part, 128), 0)

    @pl.loop(0, SECTORS)
    def _(src):
        for mm in range(4):
            for acc, (slot, vv) in zip(accs, chains):
                e = lev[src * 4 + mm, slot * VARS + step * 2 + vv]
                at = pl.ds(vv * 4 + mm, 1)
                here = jnp.broadcast_to(word[slot, src, at], (part, 128)) == words
                for g in range(GROUPS):
                    v = jnp.broadcast_to(bit[slot, g, src, at], (part, 128))
                    span = pl.ds(g * part, part)
                    acc[e, span] = acc[e, span] + jnp.where(here, v, 0)

    for k in range(0, 8, joined):
        for c in range(k, k + joined):
            for e in range(LEVELS):
                a = accs[c][e]
                accs[c][e] = jnp.zeros_like(a)
                for j in range(4):
                    n = lax.shift_right_logical(a, 8 * j) & 255
                    a_ref[c, e * 256 + j * 64 : e * 256 + j * 64 + 64] = n.astype(F32).astype(BF16)
        counts = jnp.concatenate([a_ref[c] for c in range(k, k + joined)], axis=1)
        d = jnp.dot(t_ref[chains[k][1]], counts, preferred_element_type=F32).astype(BF16)
        for i in range(joined):
            p = lax.dot_general(s_ref[...], d[:, i * 128 : i * 128 + 128], (((1,), (1,)), ((), ())), preferred_element_type=F32)
            put(*chains[k + i], p)


def outer_kernel(lev, r_ref, t_ref, s_ref, p_ref, part_ref, head_ref, tail_ref, word, bit, a_ref, *accs):
    for quad in range(2):
        unpack(quad, *(tile_of(r_ref, quad * 3 + k) for k in range(3)), word, bit)
    for acc in accs:
        acc[...] = jnp.zeros_like(acc)

    def put(k, vv, p):
        p_ref[k, vv] = p
        if k < 2:
            head_ref[k, vv] = p[:CELLS].astype(BF16)
        if k >= 6:
            tail_ref[k - 6, vv] = p[:CELLS].astype(BF16)

    @pl.loop(0, 2)
    def _(vv):
        row_sums([(k, vv) for k in range(8)], 8, lev, t_ref, s_ref, word, bit, a_ref, accs, put)
        low = p_ref[0, vv, :CELLS] + p_ref[1, vv, :CELLS] + p_ref[2, vv, :CELLS]
        part_ref[0, vv] = low
        part_ref[1, vv] = low + p_ref[3, vv, :CELLS]
        high = p_ref[5, vv, :CELLS] + p_ref[6, vv, :CELLS] + p_ref[7, vv, :CELLS]
        part_ref[2, vv] = high + p_ref[4, vv, :CELLS]
        part_ref[3, vv] = high


def inner_kernel(lev, scale, r_ref, p_ref, t_ref, s_ref, o_ref, own, word, bit, a_ref, *accs):
    unpack(0, *(tile_of(r_ref, k) for k in range(3)), word, bit)
    for acc in accs:
        acc[...] = jnp.zeros_like(acc)

    def put(k, vv, p):
        own[k, vv] = p

    row_sums([(k, vv) for vv in range(2) for k in range(4)], 4, lev, t_ref, s_ref, word, bit, a_ref, accs, put)
    rows = [(p_ref, k) for k in range(4)] + [(own, k) for k in range(4)] + [(p_ref, k) for k in range(4, 8)]

    @pl.loop(0, 2)
    def _(vv):
        factor = scale[pl.program_id(0) * 2 + vv]
        for r in range(8):
            ref, k = rows[r]
            total = ref[k, vv]
            for ref, k in rows[r + 1 : r + 5]:
                total = total + ref[k, vv]
            o_ref[r + 2, vv] = (total[:CELLS] * factor).astype(BF16)


def edge_kernel(scale, part_ref, right_ref, left_ref, done_ref, o_ref, rows, sems):
    def copy(end):
        return pltpu.make_async_copy(rows.at[pl.ds(2 * end, 2)], o_ref.at[pl.ds(10 * end, 2)], sems.at[end])

    for end in range(2):

        @pl.loop(0, VARS)
        def _(v):
            if end == 0:
                near, far = left_ref[1, v].astype(F32), left_ref[0, v].astype(F32)
                sums = part_ref[0, v] + far + near, part_ref[1, v] + near
            else:
                near, far = right_ref[0, v].astype(F32), right_ref[1, v].astype(F32)
                sums = part_ref[2, v] + near, part_ref[3, v] + near + far
            for k in range(2):
                rows[2 * end + k, v] = (sums[k] * scale[v]).astype(BF16)

        copy(end).start()
    for end in range(2):
        copy(end).wait()


def scratch(slots):
    return [
        pltpu.VMEM((slots, SECTORS, 8, 128), I32),
        pltpu.VMEM((slots, GROUPS, SECTORS, 8, 128), I32),
        pltpu.VMEM((8, FEATURES, 128), BF16),
    ] + [pltpu.VMEM((LEVELS, 64, 128), I32)] * 8


PARAMS = dict(compiler_params=pltpu.CompilerParams(vmem_limit_bytes=52 << 20))
COST = pl.CostEstimate(flops=10**10, bytes_accessed=10**7, transcendentals=0)
TABLE = pl.BlockSpec((2, BINS, FEATURES), lambda i: (i, 0, 0))


def blocks(rows, cells=CELLS):
    return pl.BlockSpec((rows, 2, cells, BINS), lambda i: (0, i, 0, 0))


def outer_rows(lev, owned, table, window):
    shape = lambda rows, cells, dtype: jax.ShapeDtypeStruct((rows, VARS, cells, BINS), dtype)
    return pl.pallas_call(
        outer_kernel,
        out_shape=[shape(8, WIDE, F32), shape(4, CELLS, F32), shape(2, CELLS, BF16), shape(2, CELLS, BF16)],
        grid=(3,),
        in_specs=[SMEM, VMEM, TABLE, VMEM],
        out_specs=[blocks(8, WIDE), blocks(4), blocks(2), blocks(2)],
        scratch_shapes=scratch(8),
        cost_estimate=COST,
        **PARAMS,
    )(lev, owned, table, window)


def inner_rows(lev, scale, owned, outer, table, window):
    return pl.pallas_call(
        inner_kernel,
        out_shape=jax.ShapeDtypeStruct((ROWS, VARS, CELLS, BINS), BF16),
        grid=(3,),
        in_specs=[SMEM, SMEM, VMEM, blocks(8, WIDE), TABLE, VMEM],
        out_specs=blocks(ROWS),
        scratch_shapes=[pltpu.VMEM((4, 2, WIDE, BINS), F32)] + scratch(4),
        cost_estimate=COST,
        **PARAMS,
    )(lev, scale, owned, outer, table, window)


def edge_rows(scale, part, right, left, done):
    anywhere = pl.BlockSpec(memory_space=pl.ANY)
    return pl.pallas_call(
        edge_kernel,
        out_shape=jax.ShapeDtypeStruct((ROWS, VARS, CELLS, BINS), BF16),
        in_specs=[SMEM, VMEM, VMEM, VMEM, anywhere],
        out_specs=anywhere,
        scratch_shapes=[pltpu.VMEM((4, VARS, CELLS, BINS), BF16), pltpu.SemaphoreType.DMA((2,))],
        input_output_aliases={4: 0},
        compiler_params=pltpu.CompilerParams(vmem_limit_bytes=EDGE_MIB << 20),
        cost_estimate=pl.CostEstimate(flops=10**6, bytes_accessed=10**6, transcendentals=0),
    )(scale, part, right, left, done)


def exchanged(x):
    return lax.all_to_all(x, "member", split_axis=0, concat_axis=0, tiled=True)


def shards(codes, exponents, centers, widths):
    sector = lax.axis_index("member")
    bands = lax.axis_size("band")
    edges = jnp.concatenate([codes[:, :4], codes[:, 8:]], axis=1)
    first = exchanged(jnp.concatenate([packed_codes(edges), packed_levels(exponents)], axis=1))
    second = exchanged(packed_codes(codes[:, 4:8]))
    table = kernel_table(centers, widths)
    lev = levels_of(first[:, 144:])
    outer_lev = jnp.concatenate([lev[:, :24], lev[:, 48:]], axis=1)
    scale = 1.0 / (25.0 * 64.0 * math.sqrt(2.0 * math.pi) * widths)
    out_l, lane = jnp.arange(WIDE)[:, None], jnp.arange(128)[None, :]
    cell = sector * CELLS + lane - 2
    window = (lane >= out_l) & (lane <= out_l + 4) & (cell >= 0) & (cell < SECTORS * CELLS) & (out_l < CELLS)
    window = window.astype(BF16)
    outer, part, head, tail = outer_rows(outer_lev, first, table, window)
    right = lax.ppermute(head, "band", [(i + 1, i) for i in range(bands - 1)])
    left = lax.ppermute(tail, "band", [(i, i + 1) for i in range(bands - 1)])
    done = inner_rows(lev[:, 24:48], scale, second, outer, table, window)
    return edge_rows(scale, part, right, left, done)


def solution(mesh):
    return jax.shard_map(
        shards,
        mesh=mesh,
        in_specs=(P("member", "band", None, None), P("member", "band", None), P(), P()),
        out_specs=P("band", None, "member", None),
        check_vma=False,
    )
```

```python
import math

import jax
import jax.numpy as jnp
from jax import lax
from jax.experimental import pallas as pl
from jax.experimental.pallas import tpu as pltpu
from jax.sharding import PartitionSpec as P

F32, BF16, I32 = jnp.float32, jnp.bfloat16, jnp.int32
SECTORS, ROWS, VARS, CELLS, BINS = 16, 12, 6, 88, 256
WIDE = 96
EDGE_MIB = 32
LEVELS = 5
FEATURES = LEVELS * 256
GROUPS = 1
SPLIT = 6
SMEM = pl.BlockSpec(memory_space=pltpu.SMEM)
VMEM = pl.BlockSpec(memory_space=pltpu.VMEM)


def packed_codes(codes):
    groups = codes.shape[1] // 4
    c = jnp.pad(codes.astype(BF16), ((0, 0), (0, 0), (0, 0), (2, WIDE - CELLS - 2)))
    s = jnp.stack([c[..., CELLS * j : CELLS * j + WIDE] for j in range(SECTORS)])
    s = s.reshape(SECTORS, 4, groups, 4, VARS, WIDE)
    s = jnp.transpose(s, (0, 2, 4, 1, 3, 5)).reshape(SECTORS, groups, VARS, 4, 3, 128)
    return jnp.transpose(s, (0, 1, 4, 2, 3, 5)).reshape(SECTORS, groups * 72, 128)


def packed_levels(exponents):
    e = jnp.pad((exponents + 8).astype(BF16).reshape(4, ROWS * VARS), ((0, 4), (0, 128 - ROWS * VARS)))
    return jnp.broadcast_to(e[None], (SECTORS, 8, 128))


def levels_of(rows):
    return rows[:, :4, : ROWS * VARS].astype(I32).reshape(4 * SECTORS, ROWS * VARS)


def kernel_table(centers, widths):
    f = jnp.arange(FEATURES)
    level, byte, word = f // 256, (f // 64) % 4, f % 64
    x = (4 * word + byte - 128).astype(F32) * jnp.exp2((level - 8).astype(F32))
    d = (centers[:, :, None] - x[None, None, :]) / widths[:, None, None]
    return jnp.exp(-0.5 * d * d).astype(BF16)


def unpack(quad, t0, t1, t2, word, bit):
    lane = lax.broadcasted_iota(I32, (SECTORS, 8, 128), 2)

    def put(k, x):
        c = x.astype(I32) + 128
        word[quad * 4 + k] = lax.shift_right_logical(c, 2)
        bit[quad * 4 + k, 0] = lax.shift_left(jnp.ones_like(c), (c & 3) * 8)

    put(0, t0)
    put(1, jnp.where(lane < 32, pltpu.roll(t0, 32, 2), pltpu.roll(t1, 32, 2)))
    put(2, jnp.where(lane < 64, pltpu.roll(t1, 64, 2), pltpu.roll(t2, 64, 2)))
    put(3, pltpu.roll(t2, 96, 2))


def tile_of(ref, k):
    start = pl.multiple_of(k * 24 + pl.program_id(0) * 8, 8)
    return ref[:, pl.ds(start, 8), :].astype(F32)


def row_sums(chains, joined, lev, t_ref, s_ref, word, bit, a_ref, accs, put):
    step = pl.program_id(0)
    part = 64 // GROUPS
    words = lax.broadcasted_iota(I32, (part, 128), 0)

    @pl.loop(0, SECTORS // 2)
    def _(pair):
        for m in range(8):
            src, mm = pair * 2 + m // 4, m % 4
            for acc, (slot, vv) in zip(accs, chains):
                e = lev[src * 4 + mm, slot * VARS + step * 2 + vv]
                at = pl.ds(vv * 4 + mm, 1)
                here = jnp.broadcast_to(word[slot, src, at], (part, 128)) == words
                for g in range(GROUPS):
                    v = jnp.broadcast_to(bit[slot, g, src, at], (part, 128))
                    span = pl.ds(g * part, part)
                    acc[e, span] = acc[e, span] + jnp.where(here, v, 0)

    for k in range(0, 8, joined):
        for c in range(k, k + joined):
            for e in range(LEVELS):
                a = accs[c][e]
                accs[c][e] = jnp.zeros_like(a)
                for j in range(4):
                    n = lax.shift_right_logical(a, 8 * j) & 255
                    a_ref[c, e * 256 + j * 64 : e * 256 + j * 64 + 64] = n.astype(F32).astype(BF16)
        counts = jnp.concatenate([a_ref[c] for c in range(k, k + joined)], axis=1)
        d = jnp.dot(t_ref[chains[k][1]], counts, preferred_element_type=F32).astype(BF16)
        for i in range(joined):
            p = lax.dot_general(s_ref[...], d[:, i * 128 : i * 128 + 128], (((1,), (1,)), ((), ())), preferred_element_type=F32)
            put(*chains[k + i], p)


def outer_kernel(lev, r_ref, t_ref, s_ref, p_ref, part_ref, head_ref, tail_ref, word, bit, a_ref, *accs):
    for quad in range(2):
        unpack(quad, *(tile_of(r_ref, quad * 3 + k) for k in range(3)), word, bit)
    for acc in accs:
        acc[...] = jnp.zeros_like(acc)

    def put(k, vv, p):
        p_ref[k, vv] = p
        if k < 2:
            head_ref[k, vv] = p[:CELLS].astype(BF16)
        if k >= 6:
            tail_ref[k - 6, vv] = p[:CELLS].astype(BF16)

    @pl.loop(0, 2)
    def _(vv):
        row_sums([(k, vv) for k in range(8)], 8, lev, t_ref, s_ref, word, bit, a_ref, accs, put)
        low = p_ref[0, vv, :CELLS] + p_ref[1, vv, :CELLS] + p_ref[2, vv, :CELLS]
        part_ref[0, vv] = low
        part_ref[1, vv] = low + p_ref[3, vv, :CELLS]
        high = p_ref[5, vv, :CELLS] + p_ref[6, vv, :CELLS] + p_ref[7, vv, :CELLS]
        part_ref[2, vv] = high + p_ref[4, vv, :CELLS]
        part_ref[3, vv] = high


def inner_kernel(lev, scale, r_ref, p_ref, t_ref, s_ref, o_ref, own, word, bit, a_ref, *accs):
    unpack(0, *(tile_of(r_ref, k) for k in range(3)), word, bit)
    for acc in accs:
        acc[...] = jnp.zeros_like(acc)

    def put(k, vv, p):
        own[k, vv] = p

    row_sums([(k, vv) for vv in range(2) for k in range(4)], 4, lev, t_ref, s_ref, word, bit, a_ref, accs, put)
    rows = [(p_ref, k) for k in range(4)] + [(own, k) for k in range(4)] + [(p_ref, k) for k in range(4, 8)]

    @pl.loop(0, 2)
    def _(vv):
        factor = scale[pl.program_id(0) * 2 + vv]
        for r in range(8):
            ref, k = rows[r]
            total = ref[k, vv]
            for ref, k in rows[r + 1 : r + 5]:
                total = total + ref[k, vv]
            o_ref[r + 2, vv] = (total[:CELLS] * factor).astype(BF16)


def edge_kernel(scale, part_ref, right_ref, left_ref, done_ref, o_ref, rows, sems):
    def copy(end):
        return pltpu.make_async_copy(rows.at[pl.ds(2 * end, 2)], o_ref.at[pl.ds(10 * end, 2)], sems.at[end])

    for end in range(2):

        @pl.loop(0, VARS)
        def _(v):
            if end == 0:
                near, far = left_ref[1, v].astype(F32), left_ref[0, v].astype(F32)
                sums = part_ref[0, v] + far + near, part_ref[1, v] + near
            else:
                near, far = right_ref[0, v].astype(F32), right_ref[1, v].astype(F32)
                sums = part_ref[2, v] + near, part_ref[3, v] + near + far
            for k in range(2):
                rows[2 * end + k, v] = (sums[k] * scale[v]).astype(BF16)

        copy(end).start()
    for end in range(2):
        copy(end).wait()


def scratch(slots):
    return [
        pltpu.VMEM((slots, SECTORS, 8, 128), I32),
        pltpu.VMEM((slots, GROUPS, SECTORS, 8, 128), I32),
        pltpu.VMEM((8, FEATURES, 128), BF16),
    ] + [pltpu.VMEM((LEVELS, 64, 128), I32)] * 8


PARAMS = dict(compiler_params=pltpu.CompilerParams(vmem_limit_bytes=52 << 20))
COST = pl.CostEstimate(flops=10**10, bytes_accessed=10**7, transcendentals=0)
TABLE = pl.BlockSpec((2, BINS, FEATURES), lambda i: (i, 0, 0))


def blocks(rows, cells=CELLS):
    return pl.BlockSpec((rows, 2, cells, BINS), lambda i: (0, i, 0, 0))


def outer_rows(lev, owned, table, window):
    shape = lambda rows, cells, dtype: jax.ShapeDtypeStruct((rows, VARS, cells, BINS), dtype)
    return pl.pallas_call(
        outer_kernel,
        out_shape=[shape(8, WIDE, F32), shape(4, CELLS, F32), shape(2, CELLS, BF16), shape(2, CELLS, BF16)],
        grid=(3,),
        in_specs=[SMEM, VMEM, TABLE, VMEM],
        out_specs=[blocks(8, WIDE), blocks(4), blocks(2), blocks(2)],
        scratch_shapes=scratch(8),
        cost_estimate=COST,
        **PARAMS,
    )(lev, owned, table, window)


def inner_rows(lev, scale, owned, outer, table, window):
    return pl.pallas_call(
        inner_kernel,
        out_shape=jax.ShapeDtypeStruct((ROWS, VARS, CELLS, BINS), BF16),
        grid=(3,),
        in_specs=[SMEM, SMEM, VMEM, blocks(8, WIDE), TABLE, VMEM],
        out_specs=blocks(ROWS),
        scratch_shapes=[pltpu.VMEM((4, 2, WIDE, BINS), F32)] + scratch(4),
        cost_estimate=COST,
        **PARAMS,
    )(lev, scale, owned, outer, table, window)


def edge_rows(scale, part, right, left, done):
    anywhere = pl.BlockSpec(memory_space=pl.ANY)
    return pl.pallas_call(
        edge_kernel,
        out_shape=jax.ShapeDtypeStruct((ROWS, VARS, CELLS, BINS), BF16),
        in_specs=[SMEM, VMEM, VMEM, VMEM, anywhere],
        out_specs=anywhere,
        scratch_shapes=[pltpu.VMEM((4, VARS, CELLS, BINS), BF16), pltpu.SemaphoreType.DMA((2,))],
        input_output_aliases={4: 0},
        compiler_params=pltpu.CompilerParams(vmem_limit_bytes=EDGE_MIB << 20),
        cost_estimate=pl.CostEstimate(flops=10**6, bytes_accessed=10**6, transcendentals=0),
    )(scale, part, right, left, done)


def exchanged(x):
    return lax.all_to_all(x, "member", split_axis=0, concat_axis=0, tiled=True)


def shards(codes, exponents, centers, widths):
    sector = lax.axis_index("member")
    bands = lax.axis_size("band")
    edges = jnp.concatenate([codes[:, :4], codes[:, 8:]], axis=1)
    first = exchanged(jnp.concatenate([packed_codes(edges), packed_levels(exponents)], axis=1))
    second = exchanged(packed_codes(codes[:, 4:8]))
    table = kernel_table(centers, widths)
    lev = levels_of(first[:, 144:])
    outer_lev = jnp.concatenate([lev[:, :24], lev[:, 48:]], axis=1)
    scale = 1.0 / (25.0 * 64.0 * math.sqrt(2.0 * math.pi) * widths)
    out_l, lane = jnp.arange(WIDE)[:, None], jnp.arange(128)[None, :]
    cell = sector * CELLS + lane - 2
    window = (lane >= out_l) & (lane <= out_l + 4) & (cell >= 0) & (cell < SECTORS * CELLS) & (out_l < CELLS)
    window = window.astype(BF16)
    outer, part, head, tail = outer_rows(outer_lev, first, table, window)
    right = lax.ppermute(head, "band", [(i + 1, i) for i in range(bands - 1)])
    left = lax.ppermute(tail, "band", [(i, i + 1) for i in range(bands - 1)])
    done = inner_rows(lev[:, 24:48], scale, second, outer, table, window)
    return edge_rows(scale, part, right, left, done)


def solution(mesh):
    return jax.shard_map(
        shards,
        mesh=mesh,
        in_specs=(P("member", "band", None, None), P("member", "band", None), P(), P()),
        out_specs=P("band", None, "member", None),
        check_vma=False,
    )
```
